512 devices in a mesh: lat: 16 (over z), lon: 32 (over x, y, core).
Axes of the slice: x: 4, y: 4, z: 16, core: 2. Of those that a mesh axis runs over, the one named last changes fastest.
Arguments:
- diffusivity: float32 [10, 512, 4096], P(None, 'lat', 'lon'), may hold values from 0.03 to 0.24
- land_mask: int32 [512, 4096], P('lat', 'lon'), may hold values 0 or 1
- obs_weights: bfloat16 [2, 8, 512, 4096], P(None, None, 'lat', 'lon'), may hold values from -0.09375 to 0.09375
- innovation: float32 [2, 16, 32, 8], P(None, 'lat', 'lon'), may hold values from -192 to 192
- precision_weights: float32 [2, 16, 32, 8], P(None, 'lat', 'lon'), may hold values from 0.5 to 4
- obs_count: int32 [16, 32], P('lat', 'lon'), may hold values from 2 to 8, as said below
Outputs:
- control: float32 [10, 512, 4096], P(None, 'lat', 'lon')
- increment: float32 [10, 512, 4096], P(None, 'lat', 'lon')
The draws below stay inside these ranges and needn't reach their ends.
Inputs may be any that keep to these rules, and one draw needn't show every extreme that they name: Tile (a, b) has valid observations in slots 0 to obs_count[a, b] - 1; some tile has 8.
All inputs are finite; a program needn't handle non-finite values. No bound on the sum of `land_mask` on one device may be relied on, other than what follows from the above.
Results may differ from the reference program's by a relative error of at most 0.0049.
Values sent between devices are 32-bit elements; how exact they have to be, the bound alone decides.
No kernel may reach another device: no remote copies, remote signals or barrier semaphores. Data moves between devices by JAX's collectives and lax.ppermute only.
A program may use at most 64 MiB of HBM per device.

```python
import math
import jax
import jax.numpy as jnp
from jax import lax

NCAT = 5
FIELDS = 10
CX = 32
CY = 128
OBS = 8
STEPS = 6
ITERS = 2
TILES_LAT = 16
TILES_LON = 32
NX = 512
NY = 4096


def draw_obs_count(key, part):
    first, second = jax.random.split(key)
    counts = jax.random.randint(first, (TILES_LAT, TILES_LON), OBS // 4, OBS + 1)
    chosen = jax.random.randint(second, (), 0, TILES_LAT * TILES_LON)
    places = lax.broadcasted_iota(jnp.int32, (TILES_LAT, TILES_LON), 0) * TILES_LON + lax.broadcasted_iota(jnp.int32, (TILES_LAT, TILES_LON), 1)
    return jnp.where(places == chosen, OBS, counts).astype(jnp.int32)


def touch_ends(result, key, low, high):
    shape = result.shape
    index_at = [jax.random.randint(jax.random.fold_in(key, axis), (), 0, shape[axis]) for axis in range(len(shape))]
    result = result.at[tuple(index_at)].set(low)
    longest = shape.index(max(shape))
    index_at[longest] = (index_at[longest] + 1) % shape[longest]
    return result.at[tuple(index_at)].set(high)


def levels(own_key, extent, cuts, least, high):
    def one(axis_at, parts):
        steps = jax.random.uniform(jax.random.fold_in(jax.random.fold_in(own_key, 6), axis_at), (parts,), jnp.float32, least / len(cuts), high / len(cuts))
        return jnp.repeat(jnp.exp(steps), extent[axis_at] // parts).reshape((-1,) + (1,) * (len(extent) - axis_at - 1))

    factor_of = one(*cuts[0])
    for cut in cuts[1:]:
        factor_of = factor_of * one(*cut)
    return factor_of


def normal_values(own_key, dims, deviation, limit, shards=(), kind=jnp.bfloat16):
    values = jax.random.normal(own_key, dims, jnp.float32) * deviation
    if len(shards) > 0:
        values = levels(own_key, dims, shards, -0.22, 0.18) * values
    return jnp.clip(values, min=-limit, max=limit).astype(kind)


def setup_inputs(seed: int = 0) -> dict:
    seeds = jax.random.split(jax.random.key(seed), 7)
    diffusivity = jnp.clip(jnp.exp(math.log(0.24) - 2.0794415 * jax.random.uniform(seeds[0], (FIELDS, NX, NY), jnp.float32) ** levels(seeds[0], (FIELDS, NX, NY), ((1, 16), (2, 32)), -0.2, 0.2)), 0.03, 0.24)
    land_mask = touch_ends((jax.random.randint(seeds[1], (NX, NY), 0, 5) < 4).astype(jnp.int32), jax.random.fold_in(seeds[1], 1), 0, 1)
    obs_weights = normal_values(seeds[2], (2, OBS, NX, NY), (CX * CY) ** -0.5, 0.09375, ((2, 16), (3, 32)))
    innovation = normal_values(seeds[3], (2, TILES_LAT, TILES_LON, OBS), 32.0, 192.0, ((1, 16), (2, 32)), jnp.float32)
    precision_weights = jnp.clip(jnp.exp(math.log(4.0) - 2.0794415 * jax.random.uniform(seeds[4], (2, TILES_LAT, TILES_LON, OBS), jnp.float32) ** levels(seeds[4], (2, TILES_LAT, TILES_LON, OBS), ((1, 16), (2, 32)), -0.2, 0.2)), 0.5, 4.0)
    obs_count = draw_obs_count(jax.random.fold_in(seeds[6], 71), 0)
    return {"diffusivity": diffusivity, "land_mask": land_mask, "obs_weights": obs_weights, "innovation": innovation, "precision_weights": precision_weights, "obs_count": obs_count}


def pad_grid(field, width):
    field = jnp.pad(field, ((0, 0), (width, width), (0, 0)))
    return jnp.concatenate([field[:, :, -width:], field, field[:, :, :width]], axis=2)


def advance(padded, east_face, north_face):
    center = padded[:, 1:-1, 1:-1]
    change = east_face[:, 1:-1, 1:] * (padded[:, 1:-1, 2:] - center)
    change = change + east_face[:, 1:-1, :-1] * (padded[:, 1:-1, :-2] - center)
    change = change + north_face[:, 1:, 1:-1] * (padded[:, 2:, 1:-1] - center)
    change = change + north_face[:, :-1, 1:-1] * (padded[:, :-2, 1:-1] - center)
    return center + change


def reference(diffusivity, land_mask, obs_weights, innovation, precision_weights, obs_count):
    ocean = land_mask.astype(jnp.float32)[None]
    scaled = pad_grid(diffusivity * ocean, 1)
    wet = pad_grid(ocean, 1)
    east = 0.5 * (scaled[:, :, :-1] * wet[:, :, 1:] + scaled[:, :, 1:] * wet[:, :, :-1])
    north = 0.5 * (scaled[:, :-1, :] * wet[:, 1:, :] + scaled[:, 1:, :] * wet[:, :-1, :])

    def diffuse(field):
        for _ in range(STEPS):
            field = advance(pad_grid(field, 1), east, north)
        return field

    def cover(field):
        return ocean * diffuse(field)

    def cover_adjoint(field):
        return diffuse(ocean * field)

    slots = lax.broadcasted_iota(jnp.int32, innovation.shape, 3)
    keep = jnp.where(slots < obs_count[None, :, :, None], precision_weights, 0.0)

    def observe(field):
        total = field.reshape(2, NCAT, NX, NY).sum(axis=1).astype(jnp.bfloat16)

        def one_row(index):
            block = lax.dynamic_slice_in_dim(obs_weights, index * CX, CX, 2).astype(jnp.float32)
            piece = lax.dynamic_slice_in_dim(total, index * CX, CX, 1).astype(jnp.float32)
            block = block.reshape(2, OBS, CX, TILES_LON, CY)
            piece = piece.reshape(2, CX, TILES_LON, CY)
            return jnp.einsum("foxby,fxby->fbo", block, piece, precision=lax.Precision.HIGHEST)

        rows = lax.map(one_row, jnp.arange(TILES_LAT, dtype=jnp.int32))
        return jnp.transpose(rows, (1, 0, 2, 3))

    def spread(weighted):
        rounded = weighted.astype(jnp.bfloat16)

        def one_row(index):
            block = lax.dynamic_slice_in_dim(obs_weights, index * CX, CX, 2).astype(jnp.float32)
            block = block.reshape(2, OBS, CX, TILES_LON, CY)
            piece = lax.dynamic_index_in_dim(rounded, index, 1, keepdims=False).astype(jnp.float32)
            back = jnp.einsum("foxby,fbo->fxby", block, piece, precision=lax.Precision.HIGHEST)
            return back.reshape(2, CX, NY)

        rows = lax.map(one_row, jnp.arange(TILES_LAT, dtype=jnp.int32))
        back = jnp.transpose(rows, (1, 0, 2, 3)).reshape(2, NX, NY)
        return jnp.repeat(back, NCAT, axis=0)

    def hessian(direction):
        return direction + cover_adjoint(spread(keep * observe(cover(direction))))

    right = cover_adjoint(spread(keep * innovation))
    control = jnp.zeros_like(right)
    residual = right
    direction = right
    norm_now = jnp.sum(residual * residual)
    for number in range(ITERS):
        image = hessian(direction)
        alpha = norm_now / jnp.sum(direction * image)
        control = control + alpha * direction
        residual = residual - alpha * image
        if number + 1 < ITERS:
            norm_next = jnp.sum(residual * residual)
            direction = residual + (norm_next / norm_now) * direction
            norm_now = norm_next
    return control, cover(control)
```

```python
import jax
import jax.numpy as jnp
from jax import lax
from jax.sharding import PartitionSpec as P

NCAT = 5
STEPS = 6
ITERS = 2


def extended(block, sides, width):
    for axis, dim in sides:
        count = lax.axis_size(axis)
        forward = [(i, i + 1) for i in range(count - 1)]
        forward.append((count - 1, 0))
        backward = [(target, source) for source, target in forward]
        low = lax.ppermute(
            lax.slice_in_dim(block, block.shape[dim] - width, None, axis=dim), axis, forward
        )
        high = lax.ppermute(lax.slice_in_dim(block, 0, width, axis=dim), axis, backward)
        block = jnp.concatenate([low, block, high], axis=dim)
    return block


def outside_rows(rows, width):
    lat_count = lax.axis_size("lat")
    lat_place = lax.axis_index("lat")
    row_ids = lax.broadcasted_iota(jnp.int32, (1, rows, 1), 1)
    return (lat_place == 0) & (row_ids < width) | (lat_place == lat_count - 1) & (
        row_ids >= rows - width
    )


def advance(padded, east_face, north_face):
    center = padded[:, 1:-1, 1:-1]
    change = east_face[:, 1:-1, 1:] * (padded[:, 1:-1, 2:] - center)
    change = change + east_face[:, 1:-1, :-1] * (padded[:, 1:-1, :-2] - center)
    change = change + north_face[:, 1:, 1:-1] * (padded[:, 2:, 1:-1] - center)
    change = change + north_face[:, :-1, 1:-1] * (padded[:, :-2, 1:-1] - center)
    return center + change


def face_pair(grown):
    scaled = grown[:-1]
    wet = grown[-1:]
    east = 0.5 * (scaled[:, :, :-1] * wet[:, :, 1:] + scaled[:, :, 1:] * wet[:, :, :-1])
    north = 0.5 * (scaled[:, :-1, :] * wet[:, 1:, :] + scaled[:, 1:, :] * wet[:, :-1, :])
    return (east, north)


def squares(residual):
    return lax.psum(jnp.sum(residual * residual), ("lat", "lon"))


def per_device(diffusivity, land_mask, obs_weights, innovation, precision_weights, obs_count):
    ocean = land_mask.astype(jnp.float32)
    tile_rows, tile_cols = ocean.shape
    width = STEPS
    stacked = jnp.concatenate([diffusivity * ocean[None], ocean[None]], axis=0)
    grown = extended(stacked, (("lat", 1), ("lon", 2)), width)
    grown = jnp.where(outside_rows(grown.shape[1], width), 0.0, grown)
    east, north = face_pair(grown)
    edge = outside_rows(tile_rows + 2 * width, width)

    def extend(field):
        field = extended(field, (("lat", 1), ("lon", 2)), width)
        return jnp.where(edge, 0.0, field)

    def diffuse(field):
        field = extend(field)
        for number in range(STEPS):
            halo = width - number
            lo = width - halo
            east_part = east[:, lo : lo + tile_rows + 2 * halo, lo : lo + tile_cols + 2 * halo - 1]
            north_part = north[:, lo : lo + tile_rows + 2 * halo - 1, lo : lo + tile_cols + 2 * halo]
            field = advance(field, east_part, north_part)
        return field

    def cover(field):
        return ocean[None] * diffuse(field)

    def cover_adjoint(field):
        return diffuse(ocean[None] * field)

    flat_weights = obs_weights.reshape(2, obs_weights.shape[1], tile_rows * tile_cols)
    slots = lax.broadcasted_iota(jnp.int32, innovation.shape, 3)
    keep = jnp.where(slots < obs_count[0, 0], precision_weights, 0.0)

    def spread(weighted):
        rounded = weighted.reshape(2, -1).astype(jnp.bfloat16)
        back = jnp.einsum("fok,fo->fk", flat_weights, rounded, preferred_element_type=jnp.float32)
        return jnp.repeat(back.reshape(2, tile_rows, tile_cols), NCAT, axis=0)

    right = cover_adjoint(spread(keep * innovation))
    control = jnp.zeros_like(right)
    residual = right
    direction = right
    norm_now = squares(residual)
    for number in range(ITERS):
        total = (
            cover(direction).reshape(2, NCAT, tile_rows, tile_cols).sum(axis=1).astype(jnp.bfloat16)
        )
        seen = jnp.einsum(
            "fok,fk->fo", flat_weights, total.reshape(2, -1), preferred_element_type=jnp.float32
        )
        image = direction + cover_adjoint(spread(keep * seen.reshape(innovation.shape)))
        alpha = norm_now / lax.psum(jnp.sum(direction * image), ("lat", "lon"))
        control = control + alpha * direction
        residual = residual - alpha * image
        if number + 1 < ITERS:
            norm_next = squares(residual)
            direction = residual + norm_next / norm_now * direction
            norm_now = norm_next
    return (control, cover(control))


def solution(mesh):
    return jax.shard_map(
        per_device,
        mesh=mesh,
        in_specs=(
            P(None, "lat", "lon"),
            P("lat", "lon"),
            P(None, None, "lat", "lon"),
            P(None, "lat", "lon", None),
            P(None, "lat", "lon", None),
            P("lat", "lon"),
        ),
        out_specs=(P(None, "lat", "lon"), P(None, "lat", "lon")),
        check_vma=False,
    )
```
